32 devices in a mesh: parts: 2 (over y), turn: 4 (over x, core), branch: 4 (over z).
Axes of the slice: x: 2, y: 2, z: 4, core: 2. Of those that a mesh axis runs over, the one named last changes fastest.
Arguments:
- query: bfloat16 [4096, 4096], P(('parts', 'turn', 'branch')), parts along dimension 0, may hold values from -128 to 128
- branch_key_value: bfloat16 [2, 4096, 512], P(None, ('parts', 'turn', 'branch')), parts along dimension 1, may hold values from -4 to 4
- turn_key_value: bfloat16 [2, 64, 512], P(None, ('parts', 'turn', 'branch')), parts along dimension 1, may hold values from -4 to 4
- kv_trunk: bfloat16 [2, 32, 512], P(None, ('parts', 'turn', 'branch')), parts along dimension 1, may hold values from -4 to 4
- grad_out: bfloat16 [4096, 4096], P(('parts', 'turn', 'branch')), parts along dimension 0, may hold values from -6 to 6
- branch_lengths: int32 [32, 4], P(('parts', 'turn', 'branch')), parts along dimension 0, may hold values from 1 to 64, 128 in all within a row
- parents: int32 [8], P('parts'), parts along dimension 0, may hold values from -1 to 2, as said below
Outputs:
- attended: bfloat16 [4096, 4096], P(('parts', 'turn', 'branch')), parts along dimension 0
- grad_query: bfloat16 [4096, 4096], P(('parts', 'turn', 'branch')), parts along dimension 0
- grad_branch_kv: bfloat16 [2, 4096, 512], P(None, ('parts', 'turn', 'branch')), parts along dimension 1
- grad_turn_kv: bfloat16 [2, 64, 512], P(None, ('parts', 'turn', 'branch')), parts along dimension 1
- grad_trunk_kv: bfloat16 [2, 32, 512], P(None, ('parts', 'turn', 'branch')), parts along dimension 1
The draws below stay inside these ranges and needn't reach their ends.
There are 2 independent parts, one for each index of `parts`. The reference program is written for one: setup_inputs(seed, part) draws one part's arguments, and reference() takes and returns one part's arrays. A program takes and returns all parts, laid end to end along the dimension named above; each array names one. Nothing has to cross between parts.
Inputs may be any that keep to these rules, and one draw needn't show every extreme that they name: parents[t] is -1 or a turn before t; parents[0] is -1 and the last turn's parent is the turn before it.
All inputs are finite; a program needn't handle non-finite values.
Results may differ from the reference program's by a relative error of at most 0.02.
Values may be sent and summed in bfloat16 or wider, within the bound.
A program may use at most 64 MiB of HBM per device.

```python
import math
import jax
import jax.numpy as jnp
import numpy as np
from jax import lax

QUERY_HEADS = 32
KEY_VALUE_HEADS = 4
HEAD_SIZE = 128
QUERY_PER_KEY = 8
NB = 4
BRANCH_DEV = 128
MOST = 64
TURNS = 4
TRUNK_TOKENS = 16
TURN_TOKENS = 32
BRANCH_TOKENS = 2048
N_BRANCH = 4


def trunk_key_rows(key):
    base_offset = jnp.clip(jax.random.normal(jax.random.fold_in(key, 11), (TRUNK_TOKENS, KEY_VALUE_HEADS * HEAD_SIZE), jnp.float32), -4.0, 4.0)
    return base_offset


def draw_kv_trunk(key, part):
    key_part = trunk_key_rows(key)
    value_portion = jnp.clip(jax.random.normal(jax.random.fold_in(key, 13), (TRUNK_TOKENS, KEY_VALUE_HEADS * HEAD_SIZE), jnp.float32), -4.0, 4.0)
    return jnp.stack([key_part, value_portion]).astype(jnp.bfloat16)


def draw_query(key, part):
    normal_part = jax.random.normal(jax.random.fold_in(key, 21), (BRANCH_TOKENS, QUERY_HEADS * HEAD_SIZE), jnp.float32)
    return jnp.clip(normal_part, -4.0, 4.0).astype(jnp.bfloat16)


def draw_parents(key, part):
    limit = jnp.arange(TURNS, dtype=jnp.int32) + 1
    drawn = jax.random.randint(jax.random.fold_in(key, 31), (TURNS,), 0, limit, dtype=jnp.int32) - 1
    position = jnp.arange(TURNS, dtype=jnp.int32)
    return jnp.where(position == TURNS - 1, jnp.int32(TURNS - 2), drawn).astype(jnp.int32)


def steps_of(key, extent, cuts, low, high):
    level, own = 1.0, jax.random.fold_in(key, 6)
    for dim, parts in cuts:
        draws = jnp.exp(jax.random.uniform(jax.random.fold_in(own, dim), (parts,), jnp.float32, low / len(cuts), high / len(cuts)))
        level = level * jnp.repeat(draws, extent[dim] // parts).reshape([-1 if axis == dim else 1 for axis in range(len(extent))])
    return level


def length_profile(number_of, total, most, skew):
    loads = [(1 << 20) // math.isqrt(rank ** skew) + 1 for rank in range(2, number_of + 1)]
    spare, holding = total - most - (number_of - 1), [1] * (number_of - 1)
    while spare > 0:
        free = [i for i in range(number_of - 1) if holding[i] < most]
        whole, budget = sum([loads[i] for i in free]), spare
        for i in free:
            extra = min(most - holding[i], max(1, budget * loads[i] // whole), spare)
            holding[i] = holding[i] + extra
            spare = spare - extra
    return np.array([most] + holding)


def ragged(own_key, amount, total, most, skew):
    if amount == 2:
        one = jax.random.randint(own_key, (), max(1, total - most), min(most, total - 1) + 1)
        return jnp.stack([one, total - one])
    tallies = jnp.asarray(length_profile(amount, total, most, skew), jnp.int32)
    pairs = (amount - 1) // 2
    giver, taker = tallies[1:1 + 2 * pairs:2], tallies[2:2 + 2 * pairs:2]
    slack = jnp.minimum(giver - 1, most - taker)
    shifted = jax.random.randint(jax.random.fold_in(own_key, 1), (pairs,), 0, 1 << 20) % (slack + 1)
    tallies = tallies.at[1:1 + 2 * pairs:2].set(giver - shifted).at[2:2 + 2 * pairs:2].set(taker + shifted)
    return tallies[jax.random.permutation(jax.random.fold_in(own_key, 2), amount)]


def bell_draw(own_key, extent, width, bound, split=(), kind=jnp.bfloat16):
    values = width * jax.random.normal(own_key, extent, jnp.float32)
    if split:
        values = values * steps_of(own_key, extent, split, -0.22, 0.18)
    return jnp.clip(values, -bound, bound).astype(kind)


def setup_inputs(seed: int = 0, part: int = 0) -> dict:
    key_list = jax.random.split(jax.random.key(seed), 8)
    part_keys = jax.random.split(jax.random.fold_in(key_list[7], part), 8)
    query = draw_query(jax.random.fold_in(jax.random.fold_in(key_list[7], part), 71), part)
    branch_key_value = bell_draw(part_keys[1], (2, BRANCH_TOKENS, KEY_VALUE_HEADS * HEAD_SIZE), 1.0, 4.0, ((1, 16),))
    turn_key_value = bell_draw(part_keys[2], (2, TURN_TOKENS, KEY_VALUE_HEADS * HEAD_SIZE), 1.0, 4.0, ((1, 16),))
    kv_trunk = draw_kv_trunk(jax.random.fold_in(jax.random.fold_in(key_list[7], part), 71), part)
    grad_out = bell_draw(part_keys[4], (BRANCH_TOKENS, QUERY_HEADS * HEAD_SIZE), 1.0, 6.0, ((0, 16),))
    branch_lengths = jax.vmap(lambda own: ragged(own, NB, BRANCH_DEV, MOST, 2))(jax.random.split(part_keys[5], (TURNS * N_BRANCH))).reshape((TURNS * N_BRANCH, NB)).astype(jnp.int32)
    parents = draw_parents(jax.random.fold_in(jax.random.fold_in(key_list[7], part), 71), part)
    return dict(query=query, branch_key_value=branch_key_value, turn_key_value=turn_key_value, kv_trunk=kv_trunk, grad_out=grad_out, branch_lengths=branch_lengths, parents=parents)


masked_score = -1e+30

def ancestry(parents, turn_count):
    position = jnp.arange(turn_count, dtype=jnp.int32)
    parent_of = parents[:, None] == position[None, :]
    start = position[:, None] == position[None, :]

    def widen(sweep, reached):
        return reached | jnp.any(reached[:, :, None] & parent_of[None, :, :], axis=1)
    return lax.fori_loop(0, turn_count, widen, start)

def visible(path_row, lengths, trunk_rows, turn_rows, turn_count, branch_rows):
    turn_length = turn_rows // turn_count
    owner_turn = jnp.arange(turn_rows, dtype=jnp.int32) // turn_length
    on_path = jnp.any((owner_turn[:, None] == jnp.arange(turn_count, dtype=jnp.int32)[None, :]) & path_row[None, :], axis=1)
    segment_ends = jnp.cumsum(lengths, dtype=jnp.int32)
    position = jnp.arange(branch_rows, dtype=jnp.int32)
    segment = lax.optimization_barrier(jnp.sum((position[:, None] >= segment_ends[None, :]).astype(jnp.int32), axis=1))
    inside = (segment[:, None] == segment[None, :]) & (position[None, :] <= position[:, None])
    leading = jnp.ones((branch_rows, trunk_rows), dtype=bool)
    middle = jnp.broadcast_to(on_path[None, :], (branch_rows, turn_rows))
    return jnp.concatenate([leading, middle, inside], axis=1)

def group_terms(query, key_rows, values, grad_out, allowed, group_index):
    query_total = query.shape[0]
    group_width = QUERY_PER_KEY * HEAD_SIZE
    softmax_scale = 1.0 / math.sqrt(HEAD_SIZE)
    start = group_index * group_width
    queries = lax.dynamic_slice_in_dim(query, start, group_width, 1).reshape(query_total, QUERY_PER_KEY, HEAD_SIZE).astype(jnp.float32)
    cotangent = lax.dynamic_slice_in_dim(grad_out, start, group_width, 1).reshape(query_total, QUERY_PER_KEY, HEAD_SIZE).astype(jnp.float32)
    head_keys = lax.dynamic_slice_in_dim(key_rows, group_index * HEAD_SIZE, HEAD_SIZE, 1).astype(jnp.float32)
    head_values = lax.dynamic_slice_in_dim(values, group_index * HEAD_SIZE, HEAD_SIZE, 1).astype(jnp.float32)
    scores = jnp.einsum('rgd,kd->grk', queries, head_keys) * softmax_scale
    scores = jnp.where(allowed[None, :, :], scores, masked_score)
    largest = lax.optimization_barrier(jnp.max(scores, axis=2, keepdims=True))
    exponent = jnp.exp(scores - largest)
    probs = exponent / lax.optimization_barrier(jnp.sum(exponent, axis=2, keepdims=True))
    rounded = lax.optimization_barrier(probs.astype(jnp.bfloat16)).astype(jnp.float32)
    attended = jnp.einsum('grk,kd->rgd', rounded, head_values).astype(jnp.bfloat16)
    attended_wide = lax.optimization_barrier(attended).astype(jnp.float32)
    delta = lax.optimization_barrier(jnp.sum(cotangent * attended_wide, axis=2))
    dprob = jnp.einsum('rgd,kd->grk', cotangent, head_values)
    dscore = (probs * (dprob - jnp.transpose(delta)[:, :, None])).astype(jnp.bfloat16)
    dscore_wide = lax.optimization_barrier(dscore).astype(jnp.float32)
    grad_query = (jnp.einsum('grk,kd->rgd', dscore_wide, head_keys) * softmax_scale).astype(jnp.bfloat16)
    grad_keys = jnp.einsum('grk,rgd->kd', dscore_wide, queries) * softmax_scale
    grad_values = jnp.einsum('grk,rgd->kd', rounded, cotangent)
    return (attended.reshape(query_total, group_width), grad_query.reshape(query_total, group_width), grad_keys, grad_values)

def device_terms(query, key_rows, values, grad_out, allowed):
    query_total = query.shape[0]
    key_total = key_rows.shape[0]
    group_width = QUERY_PER_KEY * HEAD_SIZE

    def single_group(group_index, totals):
        attended, grad_query, grad_keys, grad_values = totals
        piece_out, piece_query, piece_keys, piece_values = group_terms(query, key_rows, values, grad_out, allowed, group_index)
        attended = lax.dynamic_update_slice_in_dim(attended, piece_out, group_index * group_width, 1)
        grad_query = lax.dynamic_update_slice_in_dim(grad_query, piece_query, group_index * group_width, 1)
        grad_keys = lax.dynamic_update_slice_in_dim(grad_keys, piece_keys, group_index * HEAD_SIZE, 1)
        grad_values = lax.dynamic_update_slice_in_dim(grad_values, piece_values, group_index * HEAD_SIZE, 1)
        return (attended, grad_query, grad_keys, grad_values)
    initial_state = (jnp.zeros((query_total, QUERY_HEADS * HEAD_SIZE), jnp.bfloat16), jnp.zeros((query_total, QUERY_HEADS * HEAD_SIZE), jnp.bfloat16), jnp.zeros((key_total, KEY_VALUE_HEADS * HEAD_SIZE), jnp.float32), jnp.zeros((key_total, KEY_VALUE_HEADS * HEAD_SIZE), jnp.float32))
    return lax.fori_loop(0, KEY_VALUE_HEADS, single_group, initial_state)

def reference(query, branch_key_value, turn_key_value, kv_trunk, grad_out, branch_lengths, parents):
    block_count = TURNS * N_BRANCH
    feature_dim = KEY_VALUE_HEADS * HEAD_SIZE
    shared_rows = TRUNK_TOKENS + TURN_TOKENS
    reached = ancestry(parents, TURNS)
    shared_keys = jnp.concatenate([kv_trunk[0], turn_key_value[0]], axis=0)
    shared_values = jnp.concatenate([kv_trunk[1], turn_key_value[1]], axis=0)
    query_blocks = query.reshape(block_count, BRANCH_DEV, QUERY_HEADS * HEAD_SIZE)
    grad_blocks = grad_out.reshape(block_count, BRANCH_DEV, QUERY_HEADS * HEAD_SIZE)
    branch_blocks = jnp.swapaxes(branch_key_value.reshape(2, block_count, BRANCH_DEV, feature_dim), 0, 1)

    def one_block(totals, pieces):
        block_index, block_query, block_kv, block_grad, lengths = pieces
        turn_index = block_index // N_BRANCH
        path_row = jnp.any(reached & (jnp.arange(TURNS, dtype=jnp.int32)[:, None] == turn_index), axis=0)
        allowed = visible(path_row, lengths, TRUNK_TOKENS, TURN_TOKENS, TURNS, BRANCH_DEV)
        key_rows = jnp.concatenate([shared_keys, block_kv[0]], axis=0)
        value_rows = jnp.concatenate([shared_values, block_kv[1]], axis=0)
        attended, grad_query, grad_keys, grad_values = device_terms(block_query, key_rows, value_rows, block_grad, allowed)
        shared = jnp.stack([grad_keys[:shared_rows], grad_values[:shared_rows]])
        own = jnp.stack([grad_keys[shared_rows:], grad_values[shared_rows:]]).astype(jnp.bfloat16)
        return (totals + shared, (attended, grad_query, own))
    start = jnp.zeros((2, shared_rows, feature_dim), jnp.float32)
    pieces = (jnp.arange(block_count, dtype=jnp.int32), query_blocks, branch_blocks, grad_blocks, branch_lengths)
    totals, outputs = lax.scan(one_block, start, pieces)
    attended = outputs[0].reshape(BRANCH_TOKENS, QUERY_HEADS * HEAD_SIZE)
    grad_query = outputs[1].reshape(BRANCH_TOKENS, QUERY_HEADS * HEAD_SIZE)
    grad_branch_kv = jnp.swapaxes(outputs[2], 0, 1).reshape(2, BRANCH_TOKENS, feature_dim)
    grad_trunk_kv = totals[:, :TRUNK_TOKENS].astype(jnp.bfloat16)
    grad_turn_kv = totals[:, TRUNK_TOKENS:].astype(jnp.bfloat16)
    return (attended, grad_query, grad_branch_kv, grad_turn_kv, grad_trunk_kv)
```

```python
import functools
import math

import jax
import jax.numpy as jnp
from jax import lax
from jax.experimental import pallas as pl
from jax.experimental.pallas import tpu as pltpu
from jax.sharding import PartitionSpec as P

KEY_VALUE_HEADS = 4
HEAD_SIZE = 128
QUERY_PER_KEY = 8

masked_score = -1e30
MESH = pl.DeviceIdType.MESH
F32 = jnp.float32
BF16 = jnp.bfloat16


def dot(a, b, ca, cb):
    return lax.dot_general(a, b, (((ca,), (cb,)), ((), ())), preferred_element_type=F32)


def one_hot(cond):
    return jnp.where(cond, 1.0, 0.0).astype(BF16)


def kernel(
    turn_count, branch_count,
    query, bkv, turn_kv, trunk_kv, grad_out, lengths, parents,
    attended, grad_query, grad_branch, grad_turn, grad_trunk,
    q_v, do_v, kv_v, turn_v, trunk_v,
    pack32, pack, gathered, send, received,
    e_s, dp_s, m_s, l_s, c_s, f_s, d_s, psh_s, dssh_s, bias_s,
    ksh_s, vsh_s, o_v, dq_v, gkv_v,
    q_sem, do_sem, in_sem, own_sem, o_sem, dq_sem, gkv_sem,
    gsend_sem, grecv_sem, rsend_sem, rrecv_sem,
):
    n = turn_count * branch_count
    rows = query.shape[0]
    width = QUERY_PER_KEY * HEAD_SIZE
    pair = 2 * HEAD_SIZE
    pair_rows = 2 * rows
    pairs = QUERY_PER_KEY // 2
    trunk_own = trunk_kv.shape[1]
    turn_own = turn_kv.shape[1]
    own = trunk_own + turn_own
    trunk_rows = n * trunk_own
    turn_rows = n * turn_own
    shared = trunk_rows + turn_rows
    slot = pack.shape[0]
    half = pack.shape[1]
    scale = 1.0 / math.sqrt(HEAD_SIZE)
    log_scale = scale * math.log2(math.e)
    my_turn = lax.axis_index("turn")
    me = my_turn * branch_count + lax.axis_index("branch")

    def device(k):
        peer = lax.rem(me + k, n)
        return {"turn": lax.div(peer, branch_count), "branch": lax.rem(peer, branch_count)}

    barrier = pltpu.get_barrier_semaphore()

    def greet(k, carry):
        pl.semaphore_signal(barrier, inc=1, device_id=device(k), device_id_type=MESH)
        return carry

    lax.fori_loop(1, n, greet, 0)

    small = [
        pltpu.make_async_copy(trunk_kv, trunk_v, in_sem.at[0]),
        pltpu.make_async_copy(turn_kv, turn_v, in_sem.at[1]),
    ]
    kv_copy = pltpu.make_async_copy(bkv, kv_v, in_sem.at[2])
    for c in small:
        c.start()
    kv_copy.start()
    q_copies, do_copies = [], []
    for g in range(KEY_VALUE_HEADS):
        cols = pl.ds(g * width, width)
        q_copies.append(pltpu.make_async_copy(query.at[:, cols], q_v.at[:, cols], q_sem.at[g]))
        do_copies.append(
            pltpu.make_async_copy(grad_out.at[:, cols], do_v.at[:, cols], do_sem.at[g])
        )
        q_copies[g].start()
        do_copies[g].start()

    key_pos = lax.broadcasted_iota(jnp.int32, (rows, rows), 0)
    query_pos = lax.broadcasted_iota(jnp.int32, (rows, rows), 1)
    key_segment = jnp.zeros((rows, rows), jnp.int32)
    query_segment = jnp.zeros((rows, rows), jnp.int32)
    end = jnp.int32(0)
    for k in range(lengths.shape[1]):
        end = end + lengths[0, k]
        key_segment += jnp.where(key_pos >= end, 1, 0)
        query_segment += jnp.where(query_pos >= end, 1, 0)
    inside = (key_segment == query_segment) & (key_pos <= query_pos)
    bias_s[...] = jnp.where(inside, 0.0, masked_score)

    for c in small:
        c.wait()
    pack32[...] = jnp.zeros_like(pack32)
    for kv in range(2):
        trunk_piece = trunk_v[kv].astype(F32)
        turn_piece = turn_v[kv].astype(F32)
        for side in range(2):
            base = (kv * 2 + side) * own
            cols = slice(side * half, (side + 1) * half)
            pack32[base : base + trunk_own, :] = trunk_piece[:, cols]
            pack32[base + trunk_own : base + own, :] = turn_piece[:, cols]
    pack[...] = pack32[...].astype(BF16)

    def two(ref, g, p):
        first = g * width + p * pair
        return jnp.concatenate(
            [ref[:, first : first + HEAD_SIZE], ref[:, first + HEAD_SIZE : first + pair]], axis=0
        )

    bias2 = jnp.concatenate([bias_s[...], bias_s[...]], axis=1)

    def own_part(g):
        q_copies[g].wait()
        do_copies[g].wait()
        keys = kv_v[0, :, g * HEAD_SIZE : (g + 1) * HEAD_SIZE]
        values = kv_v[1, :, g * HEAD_SIZE : (g + 1) * HEAD_SIZE]
        for p in range(pairs):
            at = slice((g * pairs + p) * pair_rows, (g * pairs + p + 1) * pair_rows)
            scores = dot(keys, two(q_v, g, p), 1, 1) * log_scale + bias2
            largest = jnp.max(scores, axis=0, keepdims=True)
            e = jnp.exp2(scores - largest)
            dprob = dot(values, two(do_v, g, p), 1, 1)
            e_s[:, at] = e
            dp_s[:, at] = dprob
            m_s[:, at] = largest
            l_s[:, at] = jnp.sum(e, axis=0, keepdims=True)
            c_s[:, at] = jnp.sum(e * dprob, axis=0, keepdims=True)

    kv_copy.wait()

    pl.semaphore_wait(barrier, n - 1)
    mine = pl.ds(pl.multiple_of(me * slot, slot), slot)

    def give(k, carry):
        pltpu.make_async_remote_copy(
            src_ref=pack,
            dst_ref=gathered.at[mine],
            send_sem=gsend_sem,
            recv_sem=grecv_sem,
            device_id=device(k),
            device_id_type=MESH,
        ).start()
        return carry

    lax.fori_loop(1, n, give, 0)
    keep = pltpu.make_async_copy(pack, gathered.at[mine], own_sem.at[0])
    keep.start()

    for g in range(KEY_VALUE_HEADS):
        own_part(g)

    keep.wait()
    others = pl.ds(0, (n - 1) * slot)
    all_in = pltpu.make_async_remote_copy(
        src_ref=gathered.at[others],
        dst_ref=gathered.at[others],
        send_sem=gsend_sem,
        recv_sem=grecv_sem,
        device_id=device(1),
        device_id_type=MESH,
    )
    all_in.wait_recv()

    def place(shape, row_axis):
        row = lax.broadcasted_iota(jnp.int32, shape, row_axis)
        is_trunk = row < trunk_rows
        late = row - trunk_rows
        owner = jnp.where(is_trunk, row // trunk_own, late // turn_own)
        inner = jnp.where(is_trunk, row % trunk_own, late % turn_own + trunk_own)
        return owner * slot + inner

    source = place((shared, n * slot), 0)
    column = lax.broadcasted_iota(jnp.int32, (shared, n * slot), 1)
    for kv, ref in ((0, ksh_s), (1, vsh_s)):
        for side in range(2):
            pick = one_hot(column == source + (kv * 2 + side) * own)
            ref[:, side * half : (side + 1) * half] = dot(pick, gathered[...], 1, 0).astype(BF16)

    row = lax.broadcasted_iota(jnp.int32, (shared, pair_rows), 0)
    owner_turn = lax.div(row - trunk_rows, turn_rows // turn_count)
    on_path = row < trunk_rows
    current = my_turn
    for step in range(turn_count):
        on_path = on_path | ((row >= trunk_rows) & (owner_turn == current))
        parent = parents[jnp.maximum(current, 0)]
        current = jnp.where(current >= 0, parent, -1)
    shared_bias = jnp.where(on_path, 0.0, masked_score)

    key_parts, value_parts = [], []
    for g in range(KEY_VALUE_HEADS):
        head = slice(g * HEAD_SIZE, (g + 1) * HEAD_SIZE)
        keys = ksh_s[:, head]
        values = vsh_s[:, head]
        grad_keys = jnp.zeros((shared, HEAD_SIZE), F32)
        grad_values = jnp.zeros((shared, HEAD_SIZE), F32)
        for p in range(pairs):
            at = slice((g * pairs + p) * pair_rows, (g * pairs + p + 1) * pair_rows)
            queries = two(q_v, g, p)
            cotangent = two(do_v, g, p)
            scores = dot(keys, queries, 1, 1) * log_scale + shared_bias
            dprob = dot(values, cotangent, 1, 1)
            m_own = m_s[:, at]
            largest = jnp.maximum(m_own, jnp.max(scores, axis=0, keepdims=True))
            e = jnp.exp2(scores - largest)
            factor = jnp.exp2(m_own - largest)
            inverse = 1.0 / (l_s[:, at] * factor + jnp.sum(e, axis=0, keepdims=True))
            delta = (c_s[:, at] * factor + jnp.sum(e * dprob, axis=0, keepdims=True)) * inverse
            probs = e * inverse
            weights = probs.astype(BF16)
            dscore = (probs * (dprob - delta)).astype(BF16)
            f_s[:, at] = factor * inverse
            d_s[:, at] = delta
            psh_s[:, at] = weights
            dssh_s[:, at] = dscore
            grad_keys += dot(dscore, queries, 1, 0)
            grad_values += dot(weights, cotangent, 1, 0)
        key_parts.append((grad_keys * scale).astype(BF16))
        value_parts.append(grad_values.astype(BF16))

    target = place((n * slot, shared), 1)
    line = lax.broadcasted_iota(jnp.int32, (n * slot, shared), 0)
    total = jnp.zeros((n * slot, half), F32)
    per_side = KEY_VALUE_HEADS // 2
    for kv, parts in ((0, key_parts), (1, value_parts)):
        for side in range(2):
            put = one_hot(line == target + (kv * 2 + side) * own)
            piece = jnp.concatenate(parts[side * per_side : (side + 1) * per_side], axis=1)
            total += dot(put, piece, 1, 0)
    send[...] = total.astype(BF16)

    def give_back(k, carry):
        peer = lax.rem(me + k, n)
        pltpu.make_async_remote_copy(
            src_ref=send.at[pl.ds(pl.multiple_of(peer * slot, slot), slot)],
            dst_ref=received.at[mine],
            send_sem=rsend_sem,
            recv_sem=rrecv_sem,
            device_id=device(k),
            device_id_type=MESH,
        ).start()
        return carry

    lax.fori_loop(1, n, give_back, 0)
    keep = pltpu.make_async_copy(send.at[mine], received.at[mine], own_sem.at[1])
    keep.start()

    outs = []
    for g in range(KEY_VALUE_HEADS):
        head = slice(g * HEAD_SIZE, (g + 1) * HEAD_SIZE)
        keys = jnp.concatenate([kv_v[0, :, head], ksh_s[:, head]], axis=0)
        values = jnp.concatenate([kv_v[1, :, head], vsh_s[:, head]], axis=0)
        grad_keys = jnp.zeros((rows, HEAD_SIZE), F32)
        grad_values = jnp.zeros((rows, HEAD_SIZE), F32)
        for p in range(pairs):
            at = slice((g * pairs + p) * pair_rows, (g * pairs + p + 1) * pair_rows)
            probs = e_s[:, at] * f_s[:, at]
            weights = probs.astype(BF16)
            dscore = (probs * (dp_s[:, at] - d_s[:, at])).astype(BF16)
            grad_keys += dot(dscore, two(q_v, g, p), 1, 0)
            grad_values += dot(weights, two(do_v, g, p), 1, 0)
            all_weights = jnp.concatenate([weights, psh_s[:, at]], axis=0)
            all_dscore = jnp.concatenate([dscore, dssh_s[:, at]], axis=0)
            out = dot(all_weights, values, 0, 0).astype(BF16)
            out_q = (dot(all_dscore, keys, 0, 0) * scale).astype(BF16)
            first = g * width + p * pair
            for i in range(2):
                cols = slice(first + i * HEAD_SIZE, first + (i + 1) * HEAD_SIZE)
                o_v[:, cols] = out[i * rows : (i + 1) * rows]
                dq_v[:, cols] = out_q[i * rows : (i + 1) * rows]
        gkv_v[0, :, head] = (grad_keys * scale).astype(BF16)
        gkv_v[1, :, head] = grad_values.astype(BF16)
        cols = pl.ds(g * width, width)
        outs.append(pltpu.make_async_copy(o_v.at[:, cols], attended.at[:, cols], o_sem.at[g]))
        outs.append(pltpu.make_async_copy(dq_v.at[:, cols], grad_query.at[:, cols], dq_sem.at[g]))
        outs[-2].start()
        outs[-1].start()
    outs.append(pltpu.make_async_copy(gkv_v, grad_branch, gkv_sem))
    outs[-1].start()

    keep.wait()
    back_in = pltpu.make_async_remote_copy(
        src_ref=received.at[others],
        dst_ref=received.at[others],
        send_sem=rsend_sem,
        recv_sem=rrecv_sem,
        device_id=device(1),
        device_id_type=MESH,
    )
    back_in.wait_recv()
    summed = jnp.zeros((slot, half), F32)
    for d in range(n):
        summed += received[d * slot : (d + 1) * slot, :].astype(F32)
    pack32[...] = summed
    for kv in range(2):
        for side in range(2):
            base = (kv * 2 + side) * own
            cols = slice(side * half, (side + 1) * half)
            grad_trunk[kv, :, cols] = pack32[base : base + trunk_own, :].astype(BF16)
            grad_turn[kv, :, cols] = pack32[base + trunk_own : base + own, :].astype(BF16)
    all_in.wait_send()
    back_in.wait_send()
    for c in outs:
        c.wait()


def on_device(query, branch_key_value, turn_key_value, kv_trunk, grad_out, branch_lengths, parents):
    turn_count = lax.axis_size("turn")
    branch_count = lax.axis_size("branch")
    n = turn_count * branch_count
    rows, features = query.shape
    kv_width = branch_key_value.shape[2]
    own = kv_trunk.shape[1] + turn_key_value.shape[1]
    shared = n * own
    slot = -(-4 * own // 16) * 16
    half = kv_width // 2
    total = rows * (features // HEAD_SIZE)
    anywhere = pl.BlockSpec(memory_space=pl.ANY)
    scalar = pl.BlockSpec(memory_space=pltpu.SMEM)
    vector = pl.BlockSpec(memory_space=pltpu.VMEM)
    dma = pltpu.SemaphoreType.DMA
    like = lambda a: jax.ShapeDtypeStruct(a.shape, a.dtype)
    return pl.pallas_call(
        functools.partial(kernel, turn_count, branch_count),
        out_shape=(
            like(query), like(query), like(branch_key_value), like(turn_key_value), like(kv_trunk)
        ),
        in_specs=[anywhere] * 5 + [scalar, scalar],
        out_specs=(anywhere, anywhere, anywhere, vector, vector),
        scratch_shapes=[
            pltpu.VMEM(query.shape, BF16),
            pltpu.VMEM(query.shape, BF16),
            pltpu.VMEM(branch_key_value.shape, BF16),
            pltpu.VMEM(turn_key_value.shape, BF16),
            pltpu.VMEM(kv_trunk.shape, BF16),
            pltpu.VMEM((slot, half), F32),
            pltpu.VMEM((slot, half), BF16),
            pltpu.VMEM((n * slot, half), BF16),
            pltpu.VMEM((n * slot, half), BF16),
            pltpu.VMEM((n * slot, half), BF16),
            pltpu.VMEM((rows, total), F32),
            pltpu.VMEM((rows, total), F32),
            pltpu.VMEM((1, total), F32),
            pltpu.VMEM((1, total), F32),
            pltpu.VMEM((1, total), F32),
            pltpu.VMEM((1, total), F32),
            pltpu.VMEM((1, total), F32),
            pltpu.VMEM((shared, total), BF16),
            pltpu.VMEM((shared, total), BF16),
            pltpu.VMEM((rows, rows), F32),
            pltpu.VMEM((shared, kv_width), BF16),
            pltpu.VMEM((shared, kv_width), BF16),
            pltpu.VMEM(query.shape, BF16),
            pltpu.VMEM(query.shape, BF16),
            pltpu.VMEM(branch_key_value.shape, BF16),
            dma((KEY_VALUE_HEADS,)),
            dma((KEY_VALUE_HEADS,)),
            dma((3,)),
            dma((2,)),
            dma((KEY_VALUE_HEADS,)),
            dma((KEY_VALUE_HEADS,)),
            dma,
            dma,
            dma,
            dma,
            dma,
        ],
        compiler_params=pltpu.CompilerParams(collective_id=0, has_side_effects=True),
    )(query, branch_key_value, turn_key_value, kv_trunk, grad_out, branch_lengths, parents)


def solution(mesh):
    every = ("parts", "turn", "branch")
    row = P(every, None)
    middle = P(None, every, None)
    return jax.shard_map(
        on_device,
        mesh=mesh,
        in_specs=(row, middle, middle, middle, row, row, P("parts")),
        out_specs=(row, row, middle, middle, middle),
        check_vma=False,
    )
```

```python
import functools
import math

import jax
import jax.numpy as jnp
from jax import lax
from jax.experimental import pallas as pl
from jax.experimental.pallas import tpu as pltpu
from jax.sharding import PartitionSpec as P

KEY_VALUE_HEADS = 4
HEAD_SIZE = 128
QUERY_PER_KEY = 8

masked_score = -1e30
MESH = pl.DeviceIdType.MESH
F32 = jnp.float32
BF16 = jnp.bfloat16


def dot(a, b, ca, cb):
    return lax.dot_general(a, b, (((ca,), (cb,)), ((), ())), preferred_element_type=F32)


def one_hot(cond):
    return jnp.where(cond, 1.0, 0.0).astype(BF16)


def split(x, d):
    if d & (d - 1) == 0:
        return lax.shift_right_arithmetic(x, d.bit_length() - 1), x & (d - 1)
    return lax.div(x, d), lax.rem(x, d)


def kernel(
    turn_count, branch_count,
    query, bkv, turn_kv, trunk_kv, grad_out, lengths_in, parents_in,
    o_v, dq_v, gkv_v, grad_turn, grad_trunk,
    lengths, parents, q_v, do_v, kv_v, turn_v, trunk_v,
    pack32, pack, gathered, send, received, pick_s, put_s,
    e_s, dp_s, m_s, l_s, c_s, f_s, d_s, psh_s, dssh_s, bias_s, path_s,
    ksh_s, vsh_s,
    q_sem, do_sem, in_sem, own_sem,
    gsend_sem, grecv_sem, rsend_sem, rrecv_sem,
):
    n = turn_count * branch_count
    rows = query.shape[0]
    width = QUERY_PER_KEY * HEAD_SIZE
    pair = 2 * HEAD_SIZE
    pair_rows = 2 * rows
    pairs = QUERY_PER_KEY // 2
    trunk_own = trunk_kv.shape[0]
    turn_own = turn_kv.shape[1]
    own = trunk_own + turn_own
    trunk_rows = n * trunk_own
    turn_rows = n * turn_own
    shared = trunk_rows + turn_rows
    slot = pack.shape[1]
    sides = pack.shape[0]
    per_side = KEY_VALUE_HEADS // sides
    chunk = put_s.shape[1] // slot
    chunk_trunk, chunk_turn = chunk * trunk_own, chunk * turn_own
    scale = 1.0 / math.sqrt(HEAD_SIZE)
    log_scale = scale * math.log2(math.e)
    my_turn = lax.axis_index("turn")
    me = my_turn * branch_count + lax.axis_index("branch")

    def device(k):
        peer = lax.rem(me + k, n)
        return {"turn": lax.div(peer, branch_count), "branch": lax.rem(peer, branch_count)}

    barrier = pltpu.get_barrier_semaphore()

    def greet(k, carry):
        pl.semaphore_signal(barrier, inc=1, device_id=device(k), device_id_type=MESH)
        return carry

    lax.fori_loop(1, n, greet, 0)

    small = [
        pltpu.make_async_copy(trunk_kv, trunk_v, in_sem.at[0]),
        pltpu.make_async_copy(turn_kv, turn_v, in_sem.at[1]),
    ]
    scalars = [
        pltpu.make_async_copy(lengths_in, lengths, in_sem.at[3]),
        pltpu.make_async_copy(parents_in, parents, in_sem.at[4]),
    ]
    kv_copy = pltpu.make_async_copy(bkv, kv_v, in_sem.at[2])
    for c in small + scalars:
        c.start()
    kv_copy.start()
    q_copies, do_copies = [], []
    for g in range(KEY_VALUE_HEADS):
        cols = pl.ds(g * width, width)
        q_copies.append(pltpu.make_async_copy(query.at[:, cols], q_v.at[:, cols], q_sem.at[g]))
        do_copies.append(
            pltpu.make_async_copy(grad_out.at[:, cols], do_v.at[:, cols], do_sem.at[g])
        )
        q_copies[g].start()
        do_copies[g].start()

    for c in small:
        c.wait()
    pack32[...] = jnp.zeros_like(pack32)
    for kv in range(2):
        turn_piece = turn_v[kv].astype(F32)
        for g in range(KEY_VALUE_HEADS):
            base = (kv * per_side + g % per_side) * own
            cols = slice(g * HEAD_SIZE, (g + 1) * HEAD_SIZE)
            for r in range(trunk_own):
                pack32[g // per_side, base + r : base + r + 1, :] = trunk_v[r].astype(F32)[
                    kv : kv + 1, cols
                ]
            pack32[g // per_side, base + trunk_own : base + own, :] = turn_piece[:, cols]
    pack[...] = pack32[...].astype(BF16)

    def place(shape, axis):
        row = lax.broadcasted_iota(jnp.int32, shape, axis)
        trunk_owner, trunk_inner = split(row, trunk_own)
        turn_owner, turn_inner = split(row - chunk_trunk, turn_own)
        is_trunk = row < chunk_trunk
        owner = jnp.where(is_trunk, trunk_owner, turn_owner)
        return owner * slot + jnp.where(is_trunk, trunk_inner, turn_inner + trunk_own)

    chunk_shared = chunk * own
    source = place((chunk_shared, 1), 0)
    column = lax.broadcasted_iota(jnp.int32, (chunk_shared, chunk * slot), 1)
    target = place((1, chunk_shared), 1)
    line = lax.broadcasted_iota(jnp.int32, (chunk * slot, chunk_shared), 0)
    for b in range(2 * per_side):
        pick_s[b] = one_hot(column == source + b * own)
        put_s[b] = one_hot(line == target + b * own)

    def in_order(b, side):
        pieces = [
            dot(pick_s[b], gathered[side, c * chunk * slot : (c + 1) * chunk * slot], 1, 0)
            for c in range(n // chunk)
        ]
        if len(pieces) > 1:
            pieces = [x[:chunk_trunk] for x in pieces] + [x[chunk_trunk:] for x in pieces]
        return jnp.concatenate(pieces, axis=0).astype(BF16)

    def chunk_rows(x, c):
        if n == chunk:
            return x
        first = trunk_rows + c * chunk_turn
        return jnp.concatenate(
            [x[c * chunk_trunk : (c + 1) * chunk_trunk], x[first : first + chunk_turn]], axis=0
        )

    for c in scalars:
        c.wait()
    key_pos = lax.broadcasted_iota(jnp.int32, (rows, 1), 0)
    query_pos = lax.broadcasted_iota(jnp.int32, (1, rows), 1)
    key_segment = jnp.zeros((rows, 1), jnp.int32)
    query_segment = jnp.zeros((1, rows), jnp.int32)
    end = jnp.int32(0)
    for k in range(lengths.shape[1]):
        end = end + lengths[0, k]
        key_segment += jnp.where(key_pos >= end, 1, 0)
        query_segment += jnp.where(query_pos >= end, 1, 0)
    inside = (key_segment == query_segment) & (key_pos <= query_pos)
    bias_s[...] = jnp.where(inside, 0.0, masked_score)

    row = lax.broadcasted_iota(jnp.int32, (shared, HEAD_SIZE), 0)
    owner_turn, _ = split(row - trunk_rows, turn_rows // turn_count)
    on_path = row < trunk_rows
    current = my_turn
    for step in range(turn_count):
        on_path = on_path | ((row >= trunk_rows) & (owner_turn == current))
        parent = parents[jnp.maximum(current, 0)]
        current = jnp.where(current >= 0, parent, -1)
    path_s[...] = jnp.where(on_path, 0.0, masked_score)

    def two(ref, g, p):
        first = g * width + p * pair
        return jnp.concatenate(
            [ref[:, first : first + HEAD_SIZE], ref[:, first + HEAD_SIZE : first + pair]], axis=0
        )

    def own_part(g):
        q_copies[g].wait()
        do_copies[g].wait()
        keys = kv_v[0, :, g * HEAD_SIZE : (g + 1) * HEAD_SIZE]
        values = kv_v[1, :, g * HEAD_SIZE : (g + 1) * HEAD_SIZE]
        bias2 = jnp.concatenate([bias_s[...], bias_s[...]], axis=1)
        for p in range(pairs):
            at = slice((g * pairs + p) * pair_rows, (g * pairs + p + 1) * pair_rows)
            scores = dot(keys, two(q_v, g, p), 1, 1) * log_scale + bias2
            largest = jnp.max(scores, axis=0, keepdims=True)
            e = jnp.exp2(scores - largest)
            dprob = dot(values, two(do_v, g, p), 1, 1)
            e_s[:, at] = e
            dp_s[:, at] = dprob
            m_s[:, at] = largest
            l_s[:, at] = jnp.sum(e, axis=0, keepdims=True)
            c_s[:, at] = jnp.sum(e * dprob, axis=0, keepdims=True)

    pl.semaphore_wait(barrier, n - 1)
    mine = pl.ds(pl.multiple_of(me * slot, slot), slot)
    others = pl.ds(0, (n - 1) * slot)

    keeps, all_in = [], []
    for side in range(sides):

        def give(k, carry, side=side):
            pltpu.make_async_remote_copy(
                src_ref=pack.at[side],
                dst_ref=gathered.at[side, mine],
                send_sem=gsend_sem.at[side],
                recv_sem=grecv_sem.at[side],
                device_id=device(k),
                device_id_type=MESH,
            ).start()
            return carry

        lax.fori_loop(1, n, give, 0)
        keeps.append(
            pltpu.make_async_copy(pack.at[side], gathered.at[side, mine], own_sem.at[side])
        )
        keeps[side].start()
        all_in.append(
            pltpu.make_async_remote_copy(
                src_ref=gathered.at[side, others],
                dst_ref=gathered.at[side, others],
                send_sem=gsend_sem.at[side],
                recv_sem=grecv_sem.at[side],
                device_id=device(1),
                device_id_type=MESH,
            )
        )

    kv_copy.wait()
    for g in range(KEY_VALUE_HEADS):
        own_part(g)

    back_in, keeps_back = [], []
    for side in range(sides):
        keeps[side].wait()
        all_in[side].wait_recv()
        placed = [in_order(b, side) for b in range(2 * per_side)]
        for i in range(per_side):
            g = side * per_side + i
            head = slice(g * HEAD_SIZE, (g + 1) * HEAD_SIZE)
            ksh_s[:, head] = placed[i]
            vsh_s[:, head] = placed[per_side + i]

        shared_bias = jnp.concatenate([path_s[...]] * (pair_rows // HEAD_SIZE), axis=1)
        key_grads, value_grads = [], []
        for i in range(per_side):
            g = side * per_side + i
            keys = placed[i]
            values = placed[per_side + i]
            grad_keys = jnp.zeros((shared, HEAD_SIZE), F32)
            grad_values = jnp.zeros((shared, HEAD_SIZE), F32)
            for p in range(pairs):
                at = slice((g * pairs + p) * pair_rows, (g * pairs + p + 1) * pair_rows)
                queries = two(q_v, g, p)
                cotangent = two(do_v, g, p)
                scores = dot(keys, queries, 1, 1) * log_scale + shared_bias
                dprob = dot(values, cotangent, 1, 1)
                m_own = m_s[:, at]
                largest = jnp.maximum(m_own, jnp.max(scores, axis=0, keepdims=True))
                e = jnp.exp2(scores - largest)
                factor = jnp.exp2(m_own - largest)
                inverse = 1.0 / (l_s[:, at] * factor + jnp.sum(e, axis=0, keepdims=True))
                delta = (c_s[:, at] * factor + jnp.sum(e * dprob, axis=0, keepdims=True)) * inverse
                probs = e * inverse
                weights = probs.astype(BF16)
                dscore = (probs * (dprob - delta)).astype(BF16)
                f_s[:, at] = factor * inverse
                d_s[:, at] = delta
                psh_s[:, at] = weights
                dssh_s[:, at] = dscore
                grad_keys += dot(dscore, queries, 1, 0)
                grad_values += dot(weights, cotangent, 1, 0)
            key_grads.append((grad_keys * scale).astype(BF16))
            value_grads.append(grad_values.astype(BF16))
        for c in range(n // chunk):
            total = jnp.zeros((chunk * slot, HEAD_SIZE), F32)
            for b, x in enumerate(key_grads + value_grads):
                total += dot(put_s[b], chunk_rows(x, c), 1, 0)
            send[side, c * chunk * slot : (c + 1) * chunk * slot] = total.astype(BF16)

        def give_back(k, carry, side=side):
            peer = lax.rem(me + k, n)
            pltpu.make_async_remote_copy(
                src_ref=send.at[side, pl.ds(pl.multiple_of(peer * slot, slot), slot)],
                dst_ref=received.at[side, mine],
                send_sem=rsend_sem.at[side],
                recv_sem=rrecv_sem.at[side],
                device_id=device(k),
                device_id_type=MESH,
            ).start()
            return carry

        lax.fori_loop(1, n, give_back, 0)
        keeps_back.append(
            pltpu.make_async_copy(
                send.at[side, mine], received.at[side, mine], own_sem.at[sides + side]
            )
        )
        keeps_back[side].start()
        back_in.append(
            pltpu.make_async_remote_copy(
                src_ref=received.at[side, others],
                dst_ref=received.at[side, others],
                send_sem=rsend_sem.at[side],
                recv_sem=rrecv_sem.at[side],
                device_id=device(1),
                device_id_type=MESH,
            )
        )

    for g in range(KEY_VALUE_HEADS):
        head = slice(g * HEAD_SIZE, (g + 1) * HEAD_SIZE)
        keys = jnp.concatenate([kv_v[0, :, head], ksh_s[:, head]], axis=0)
        values = jnp.concatenate([kv_v[1, :, head], vsh_s[:, head]], axis=0)
        grad_keys = jnp.zeros((rows, HEAD_SIZE), F32)
        grad_values = jnp.zeros((rows, HEAD_SIZE), F32)
        for p in range(pairs):
            at = slice((g * pairs + p) * pair_rows, (g * pairs + p + 1) * pair_rows)
            probs = e_s[:, at] * f_s[:, at]
            weights = probs.astype(BF16)
            dscore = (probs * (dp_s[:, at] - d_s[:, at])).astype(BF16)
            grad_keys += dot(dscore, two(q_v, g, p), 1, 0)
            grad_values += dot(weights, two(do_v, g, p), 1, 0)
            all_weights = jnp.concatenate([weights, psh_s[:, at]], axis=0)
            all_dscore = jnp.concatenate([dscore, dssh_s[:, at]], axis=0)
            out = dot(all_weights, values, 0, 0).astype(BF16)
            out_q = (dot(all_dscore, keys, 0, 0) * scale).astype(BF16)
            first = g * width + p * pair
            for i in range(2):
                cols = slice(first + i * HEAD_SIZE, first + (i + 1) * HEAD_SIZE)
                o_v[:, cols] = out[i * rows : (i + 1) * rows]
                dq_v[:, cols] = out_q[i * rows : (i + 1) * rows]
        gkv_v[0, :, head] = (grad_keys * scale).astype(BF16)
        gkv_v[1, :, head] = grad_values.astype(BF16)

    for side in range(sides):
        keeps_back[side].wait()
        back_in[side].wait_recv()
        summed = jnp.zeros((slot, HEAD_SIZE), F32)
        for d in range(n):
            summed += received[side, d * slot : (d + 1) * slot, :].astype(F32)
        pack32[side] = summed
        for i in range(per_side):
            g = side * per_side + i
            cols = slice(g * HEAD_SIZE, (g + 1) * HEAD_SIZE)
            for kv in range(2):
                base = (kv * per_side + i) * own
                grad_turn[kv, :, cols] = pack32[side, base + trunk_own : base + own, :].astype(BF16)
            for r in range(trunk_own):
                key_at, value_at = i * own + r, (per_side + i) * own + r
                grad_trunk[r, :, cols] = jnp.concatenate(
                    [pack32[side, key_at : key_at + 1, :], pack32[side, value_at : value_at + 1, :]],
                    axis=0,
                ).astype(BF16)
    for side in range(sides):
        all_in[side].wait_send()
        back_in[side].wait_send()


def put_out(*refs):
    count = len(refs) // 2
    sems = refs[-1]
    copies = [
        pltpu.make_async_copy(refs[i], refs[count + i], sems.at[i]) for i in range(count)
    ]
    for c in copies:
        c.start()
    for c in copies:
        c.wait()


def on_device(query, branch_key_value, turn_key_value, kv_trunk, grad_out, branch_lengths, parents):
    turn_count = lax.axis_size("turn")
    branch_count = lax.axis_size("branch")
    n = turn_count * branch_count
    rows, features = query.shape
    kv_width = branch_key_value.shape[2]
    trunk = jnp.transpose(kv_trunk, (1, 0, 2))
    own = trunk.shape[0] + turn_key_value.shape[1]
    shared = n * own
    sides = 2
    per_side = KEY_VALUE_HEADS // sides
    slot = -(-2 * per_side * own // 16) * 16
    total = rows * (features // HEAD_SIZE)
    chunk = math.gcd(n, 16)
    anywhere = pl.BlockSpec(memory_space=pl.ANY)
    vector = pl.BlockSpec(memory_space=pltpu.VMEM)
    dma = pltpu.SemaphoreType.DMA
    results = (query, query, branch_key_value, turn_key_value, trunk)
    staged = pl.pallas_call(
        functools.partial(kernel, turn_count, branch_count),
        out_shape=tuple(pltpu.VMEM(a.shape, a.dtype) for a in results),
        in_specs=[anywhere] * 7,
        out_specs=(vector,) * 5,
        scratch_shapes=[
            pltpu.SMEM(branch_lengths.shape, jnp.int32),
            pltpu.SMEM(parents.shape, jnp.int32),
            pltpu.VMEM(query.shape, BF16),
            pltpu.VMEM(query.shape, BF16),
            pltpu.VMEM(branch_key_value.shape, BF16),
            pltpu.VMEM(turn_key_value.shape, BF16),
            pltpu.VMEM(trunk.shape, BF16),
            pltpu.VMEM((sides, slot, HEAD_SIZE), F32),
            pltpu.VMEM((sides, slot, HEAD_SIZE), BF16),
            pltpu.VMEM((sides, n * slot, HEAD_SIZE), BF16),
            pltpu.VMEM((sides, n * slot, HEAD_SIZE), BF16),
            pltpu.VMEM((sides, n * slot, HEAD_SIZE), BF16),
            pltpu.VMEM((2 * per_side, chunk * own, chunk * slot), BF16),
            pltpu.VMEM((2 * per_side, chunk * slot, chunk * own), BF16),
            pltpu.VMEM((rows, total), F32),
            pltpu.VMEM((rows, total), F32),
            pltpu.VMEM((1, total), F32),
            pltpu.VMEM((1, total), F32),
            pltpu.VMEM((1, total), F32),
            pltpu.VMEM((1, total), F32),
            pltpu.VMEM((1, total), F32),
            pltpu.VMEM((shared, total), BF16),
            pltpu.VMEM((shared, total), BF16),
            pltpu.VMEM((rows, rows), F32),
            pltpu.VMEM((shared, HEAD_SIZE), F32),
            pltpu.VMEM((shared, kv_width), BF16),
            pltpu.VMEM((shared, kv_width), BF16),
            dma((KEY_VALUE_HEADS,)),
            dma((KEY_VALUE_HEADS,)),
            dma((5,)),
            dma((2 * sides,)),
            dma((sides,)),
            dma((sides,)),
            dma((sides,)),
            dma((sides,)),
        ],
        compiler_params=pltpu.CompilerParams(
            collective_id=0, has_side_effects=True, vmem_limit_bytes=48 * 2**20
        ),
    )(
        *(
            pltpu.with_memory_space_constraint(a, pltpu.HBM)
            for a in (
                query, branch_key_value, turn_key_value, trunk, grad_out, branch_lengths, parents
            )
        )
    )
    outs = pl.pallas_call(
        put_out,
        out_shape=tuple(jax.ShapeDtypeStruct(a.shape, a.dtype) for a in results),
        in_specs=[vector] * 5,
        out_specs=(anywhere,) * 5,
        scratch_shapes=[dma((5,))],
        compiler_params=pltpu.CompilerParams(vmem_limit_bytes=2**20),
    )(*staged)
    return outs[:4] + (jnp.transpose(outs[4], (1, 0, 2)),)


def solution(mesh):
    every = ("parts", "turn", "branch")
    row = P(every, None)
    middle = P(None, every, None)
    return jax.shard_map(
        on_device,
        mesh=mesh,
        in_specs=(row, middle, middle, middle, row, row, P("parts")),
        out_specs=(row, row, middle, middle, middle),
        check_vma=False,
    )
```
